256 devices in a mesh: depth: 2 (over core), row: 8 (over y_lo, x), col: 16 (over z, y_hi).
Axes of the slice: x: 4, y: 4 (y_hi: 2, y_lo: 2; y = y_hi * 2 + y_lo), z: 8, core: 2. Of those that a mesh axis runs over, the one named last changes fastest.
Arguments:
- a_blocks: float32 [64, 32, 4096], P('row', 'col'), may hold values from -0.75 to 0.75
- a_index: int32 [64, 32], P('row', 'col'), may hold values from -1 to 1023, as said below
- b_blocks: float32 [256, 16, 4096], P('col', 'row'), may hold values from -6 to 6
- b_index: int32 [256, 16], P('col', 'row'), may hold values from -1 to 1023, as said below
- c_index: int32 [64, 64], P('row', 'col'), may hold values from -1 to 15, as said below
Outputs:
- c_blocks: float32 [64, 64, 4096], P('row', 'col')
The draws below stay inside these ranges and needn't reach their ends.
Inputs may be any that keep to these rules, and one draw needn't show every extreme that they name: `a_index`: slots j * 2 to (j + 1) * 2 - 1 of a block row hold block columns of k-panel j, that is j * 64 to (j + 1) * 64 - 1, or -1; the block columns of one row are distinct. Every slot group of some block rows is full. `b_index`: slots i * 2 to (i + 1) * 2 - 1 of a block column hold block rows i * 128 to (i + 1) * 128 - 1, or -1; the block rows of one column are distinct. Every slot group of some block columns is full. `c_index`: the kept block columns of one slot group of a row are distinct. Every slot group of some block rows is full.
All inputs are finite; a program needn't handle non-finite values.
Results may differ from the reference program's by a relative error of at most 0.0003.
Values sent between devices are 32-bit elements; how exact they have to be, the bound alone decides.
A program may use at most 128 MiB of HBM per device.

```python
import jax
import jax.numpy as jnp
from jax import lax

BS = 64
KB = 1024
MB_DEV = 8
NW_DEV = 16
SA = 2
SB = 2
SC = 4
MB = 64
NW = 256
KP = 64
KQ = 128
N_ROW = 8
N_COL = 16


window_span = 8


def pick_distinct(key, pool, take_count):
    pool_width = pool.shape[-1]
    scores = jax.random.randint(key, pool.shape, 0, 1 << 20) * pool_width + jnp.arange(pool_width, dtype=jnp.int32)
    ranking = jnp.argsort(scores, axis=-1, stable=True)[..., :take_count]
    return jnp.take_along_axis(pool, ranking, axis=-1)


def live_mask(key, lead_rows, others, offset):
    threshold_draw = jax.random.randint(key, (lead_rows,) + others, 0, lead_rows)
    limits = (jnp.arange(lead_rows) + offset).reshape((lead_rows,) + (1,) * len(others))
    return threshold_draw < limits


def draw_a_index(key, part):
    panels = KB // KP
    rows = jnp.arange(MB, dtype=jnp.int32)
    centers = rows % MB_DEV * KP // MB_DEV
    offsets = jnp.arange(window_span, dtype=jnp.int32)
    where_in = (centers[:, None, None] - window_span // 2 + offsets[None, None, :]) % KP
    pool = where_in + (jnp.arange(panels, dtype=jnp.int32) * KP)[None, :, None]
    picked = pick_distinct(jax.random.fold_in(key, 21), pool, SA)
    is_live = live_mask(jax.random.fold_in(key, 22), MB, (panels, SA), MB // 3)
    return jnp.where(is_live, picked, -1).reshape(MB, panels * SA).astype(jnp.int32)


def draw_b_index(key, part):
    panels = KB // KQ
    inside = KQ // KP
    columns = jnp.arange(NW, dtype=jnp.int32)
    centers = columns % NW_DEV * KP // NW_DEV
    offsets = jnp.arange(window_span, dtype=jnp.int32)
    where_in = (centers[:, None, None, None] - window_span // 2 + offsets[None, None, None, :]) % KP
    bases = (jnp.arange(panels, dtype=jnp.int32)[:, None] * inside + jnp.arange(inside, dtype=jnp.int32)[None, :]) * KP
    pool = (where_in + bases[None, :, :, None]).reshape(NW, panels, inside * window_span)
    picked = pick_distinct(jax.random.fold_in(key, 31), pool, SB)
    is_live = live_mask(jax.random.fold_in(key, 32), NW, (panels, SB), NW // 3)
    return jnp.where(is_live, picked, -1).reshape(NW, panels * SB).astype(jnp.int32)


def draw_c_index(key, part):
    panels = NW // NW_DEV
    spread = min(SC + 2, NW_DEV)
    rows = jnp.arange(MB, dtype=jnp.int32)
    centers = rows % MB_DEV * NW_DEV // MB_DEV
    offsets = jnp.arange(spread, dtype=jnp.int32)
    near = (centers[:, None, None] - spread // 2 + offsets[None, None, :]) % NW_DEV
    pool = jnp.broadcast_to(near, (MB, panels, spread))
    picked = pick_distinct(jax.random.fold_in(key, 41), pool, SC)
    is_live = live_mask(jax.random.fold_in(key, 42), MB, (panels, SC), MB // 2)
    return jnp.where(is_live, picked, -1).reshape(MB, panels * SC).astype(jnp.int32)


def block_scale(stream_key, extent, cuts, smallest, top_value):
    def one(position, shards_of):
        draws = jax.random.uniform(jax.random.fold_in(jax.random.fold_in(stream_key, 6), position), (shards_of,), jnp.float32, smallest / len(cuts), top_value / len(cuts))
        return jnp.repeat(jnp.exp(draws), extent[position] // shards_of).reshape((-1,) + (1,) * (len(extent) - position - 1))

    loudness = one(*cuts[0])
    for cut in cuts[1:]:
        loudness = loudness * one(*cut)
    return loudness


def gaussian(stream_key, extent, width, reach, split=(), kind=jnp.bfloat16):
    array = width * jax.random.normal(stream_key, extent, jnp.float32)
    if split:
        array = array * block_scale(stream_key, extent, split, -0.22, 0.18)
    return jnp.clip(array, -reach, reach).astype(kind)


def setup_inputs(seed: int = 0) -> dict:
    arg_keys = jax.random.split(jax.random.key(seed), 6)
    return {
        "a_blocks": gaussian(arg_keys[0], (MB, N_COL * SA, BS * BS), BS ** -0.5, 0.75, ((0, 8), (1, 16)), jnp.float32),
        "a_index": draw_a_index(jax.random.fold_in(arg_keys[5], 71), 0),
        "b_blocks": gaussian(arg_keys[2], (NW, N_ROW * SB, BS * BS), 1.0, 6.0, ((0, 16), (1, 8)), jnp.float32),
        "b_index": draw_b_index(jax.random.fold_in(arg_keys[5], 71), 0),
        "c_index": draw_c_index(jax.random.fold_in(arg_keys[5], 71), 0),
    }


def reference(a_blocks, a_index, b_blocks, b_index, c_index):
    slots_b = b_index.shape[1]
    slots_a = a_index.shape[1]
    slots_c = c_index.shape[1]
    valid_b = b_index >= 0
    target = jnp.where(valid_b, b_index, KB).astype(jnp.int32)
    row_ids = jnp.broadcast_to(jnp.arange(NW, dtype=jnp.int32)[:, None], b_index.shape)
    slot_ids = jnp.broadcast_to(jnp.arange(slots_b, dtype=jnp.int32)[None, :], b_index.shape)
    pos_b = jnp.full((NW, KB + 1), -1, jnp.int32).at[row_ids, target].set(slot_ids)[:, :KB]
    b_four = b_blocks.reshape(NW, slots_b, BS, BS)
    group_ids = (jnp.arange(slots_c, dtype=jnp.int32) // SC).astype(jnp.int32)

    def one_row(packed):
        a_row, a_idx, c_idx = packed
        n_glob = jnp.where(c_idx >= 0, group_ids * NW_DEV + c_idx, 0).astype(jnp.int32)
        k_safe = jnp.where(a_idx >= 0, a_idx, 0).astype(jnp.int32)
        u_ids = pos_b[n_glob[:, None], k_safe[None, :]]
        usable = (c_idx >= 0)[:, None] & (a_idx >= 0)[None, :] & (u_ids >= 0)
        chosen = b_four[n_glob[:, None], jnp.where(usable, u_ids, 0).astype(jnp.int32)]
        chosen = jnp.where(usable[:, :, None, None], chosen, jnp.zeros((), chosen.dtype))
        a_four = a_row.reshape(slots_a, BS, BS)
        result = jnp.einsum("sac,tscx->tax", a_four, chosen, precision=lax.Precision.HIGHEST)
        return result.reshape(slots_c, BS * BS)

    return lax.map(one_row, (a_blocks, a_index, c_index))
```

```python
import jax
import jax.numpy as jnp
from jax import lax
from jax.experimental import pallas as pl
from jax.experimental.pallas import tpu as pltpu
from jax.sharding import PartitionSpec as P

BS = 64
LANES = 128
ROWS = 8
COLS = 16
A_DATA = ROWS * BS
A_CHUNK = A_DATA + ROWS * 2
B_DATA = COLS * 4
B_CHUNK = B_DATA + 1
A_HALF = A_CHUNK // 2
B_PARTS = ((0, B_DATA // 2 + 1), (B_DATA // 2 + 1, B_DATA // 2))
X, Z = 4, 8
MESH = pl.DeviceIdType.MESH


def halves(x0, x1, left):
    return (
        jnp.where(left, x0, pltpu.roll(x1, BS, 1)),
        jnp.where(left, pltpu.roll(x0, BS, 1), x1),
    )


def kernel(
    a_ref, ai_ref, b_ref, bi_ref, ci_ref, o_ref,
    abuf, bbuf, pbuf, rbuf,
    asend, arecv, bsend, brecv, csend, crecv,
):
    d = lax.axis_index("depth")
    row = lax.axis_index("row")
    col = lax.axis_index("col")
    x, yl = row % X, row // X
    z, yh = col // 2, col % 2

    def at_z(step):
        return {"depth": d, "row": row, "col": ((z + step + Z) % Z) * 2 + yh}

    def at_x(step):
        return {"depth": d, "row": yl * X + (x + step + X) % X, "col": col}

    yh_peer = {"depth": d, "row": row, "col": z * 2 + (1 - yh)}
    yl_peer = {"depth": d, "row": (1 - yl) * X + x, "col": col}
    core_peer = {"depth": 1 - d, "row": row, "col": col}

    barrier = pltpu.get_barrier_semaphore()
    for peer in (at_z(1), at_z(-1), at_x(1), at_x(-1), yh_peer, yl_peer, core_peer):
        pl.semaphore_signal(barrier, inc=1, device_id=peer, device_id_type=MESH)

    a_even = (z + d) % 2 == 0
    b_even = (x + d) % 2 == 0
    left = lax.broadcasted_iota(jnp.int32, (1, LANES), 1) < BS

    def a_slot(step):
        return ((z + step + Z) % Z) // 2

    def b_slot(step):
        return ((x + step + X) % X) // 2

    @pl.when(a_even)
    def _():
        slot = a_slot(0)
        for m in range(ROWS):
            x0 = a_ref[pl.ds(m * BS, 32, stride=2), :]
            x1 = a_ref[pl.ds(m * BS + 1, 32, stride=2), :]
            low, high = halves(x0, x1, left)
            abuf[slot, yh, pl.ds(m * BS, 32), :] = low
            abuf[slot, yh, pl.ds(m * BS + 32, 32), :] = high
            for s in range(2):
                v = jnp.full((1, LANES), ai_ref[m, s])
                v = jnp.where(v < 0, -1, v + 1).astype(jnp.float32)
                abuf[slot, yh, pl.ds(A_DATA + m * 2 + s, 1), :] = v

    @pl.when(b_even)
    def _():
        slot = b_slot(0)
        for n in range(COLS):
            x0 = b_ref[pl.ds(n * BS, 32, stride=2), :]
            x1 = b_ref[pl.ds(n * BS + 1, 32, stride=2), :]
            low, high = halves(x0, x1, left)
            for g in range(4):
                bbuf[yl, slot, n * 4 + g, pl.ds(0, 8, stride=2), :] = low[g * 8 : g * 8 + 8]
                bbuf[yl, slot, n * 4 + g, pl.ds(1, 8, stride=2), :] = high[g * 8 : g * 8 + 8]
            v0 = jnp.full((1, LANES), bi_ref[n, 0])
            v1 = jnp.full((1, LANES), bi_ref[n, 1])
            v = (jnp.where(left, v0, v1) + 1).astype(jnp.float32)
            bbuf[yl, slot, B_DATA, n : n + 1, :] = v

    pl.semaphore_wait(barrier, 7)

    def a_copy(slot, sub, to, nth, part=None):
        view = abuf.at[slot, sub]
        if part is not None:
            view = abuf.at[slot, sub, pl.ds(part * A_HALF, A_HALF), :]
        return pltpu.make_async_remote_copy(
            src_ref=view, dst_ref=view,
            send_sem=asend.at[nth], recv_sem=arecv.at[slot, sub, part or 0],
            device_id=to, device_id_type=MESH,
        )

    def b_copy(slot, sub, to, nth, part=None):
        view = bbuf.at[sub, slot]
        if part is not None:
            view = bbuf.at[sub, slot, pl.ds(*B_PARTS[part])]
        return pltpu.make_async_remote_copy(
            src_ref=view, dst_ref=view,
            send_sem=bsend.at[nth], recv_sem=brecv.at[sub, slot, part or 0],
            device_id=to, device_id_type=MESH,
        )

    def a_arrived(step, sub, part=None):
        a_copy(a_slot(step), sub, at_z(1), 0, part).wait_recv()

    def b_arrived(step, sub, part=None):
        b_copy(b_slot(step), sub, at_x(1), 0, part).wait_recv()

    mine, other = yh, 1 - yh
    bmine, bother = yl, 1 - yl
    a_own = [
        a_copy(a_slot(0), mine, yh_peer, 0),
        a_copy(a_slot(0), mine, at_z(1), 1),
        a_copy(a_slot(0), mine, at_z(-1), 2),
    ]
    a_swapped = [a_copy(a_slot(0), other, at_z(1), 3), a_copy(a_slot(0), other, at_z(-1), 4)]
    even = [
        [a_copy(a_slot(-2), s, at_z(1), 5 + 2 * i), a_copy(a_slot(2), s, at_z(-1), 6 + 2 * i)]
        for i, s in enumerate((mine, other))
    ]
    odd = [
        [a_copy(a_slot(-1), s, at_z(1), 2 * i), a_copy(a_slot(1), s, at_z(-1), 1 + 2 * i)]
        for i, s in enumerate((mine, other))
    ]
    odd_far = [
        [a_copy(a_slot(-3), s, at_z(1), 4 + 2 * i, 0), a_copy(a_slot(3), s, at_z(-1), 5 + 2 * i, 1)]
        for i, s in enumerate((mine, other))
    ]
    b_own = [
        b_copy(b_slot(0), bmine, yl_peer, 0),
        b_copy(b_slot(0), bmine, at_x(1), 1),
        b_copy(b_slot(0), bmine, at_x(-1), 2),
    ]
    b_swapped = [b_copy(b_slot(0), bother, at_x(1), 3), b_copy(b_slot(0), bother, at_x(-1), 4)]
    b_far = [
        [b_copy(b_slot(-1), s, at_x(1), 2 * i, 0), b_copy(b_slot(1), s, at_x(-1), 1 + 2 * i, 1)]
        for i, s in enumerate((bmine, bother))
    ]

    def start(copies):
        for c in copies:
            c.start()

    def forward(arrived, distance, sub, copies):
        for step, c in zip((-distance, distance), copies):
            arrived(step, sub)
            c.start()

    @pl.when(a_even)
    def _():
        start(a_own)

    @pl.when(b_even)
    def _():
        start(b_own)

    @pl.when(a_even)
    def _():
        a_arrived(0, other)
        start(a_swapped)

    @pl.when(jnp.logical_not(a_even))
    def _():
        forward(a_arrived, 1, mine, odd[0])

    @pl.when(b_even)
    def _():
        b_arrived(0, bother)
        start(b_swapped)

    @pl.when(jnp.logical_not(b_even))
    def _():
        forward(b_arrived, 1, bmine, b_far[0])

    @pl.when(a_even)
    def _():
        forward(a_arrived, 2, mine, even[0])

    @pl.when(jnp.logical_not(a_even))
    def _():
        forward(a_arrived, 1, other, odd[1])
        forward(a_arrived, 3, mine, odd_far[0])

    @pl.when(a_even)
    def _():
        forward(a_arrived, 2, other, even[1])

    @pl.when(jnp.logical_not(b_even))
    def _():
        forward(b_arrived, 1, bother, b_far[1])

    @pl.when(jnp.logical_not(a_even))
    def _():
        forward(a_arrived, 3, other, odd_far[1])

    @pl.when(a_even)
    def _():
        for sub in (mine, other):
            for part in range(2):
                a_arrived(4, sub, part)

    @pl.when(b_even)
    def _():
        for sub in (bmine, bother):
            for part in range(2):
                b_arrived(2, sub, part)

    def c_copy(m):
        rows = pl.ds(pl.multiple_of(m * LANES, LANES), LANES)
        return pltpu.make_async_remote_copy(
            src_ref=pbuf.at[rows, :], dst_ref=rbuf.at[rows, :],
            send_sem=csend.at[m], recv_sem=crecv.at[m],
            device_id=core_peer, device_id_type=MESH,
        )

    def one_row(m, carry):
        base = pl.multiple_of(m * BS, BS)
        column = lax.broadcasted_iota(jnp.int32, (COLS, LANES), 0)
        wanted = [ci_ref[m, t] for t in range(4)]
        total = jnp.zeros((BS, 4 * BS), jnp.float32)
        for zs in range(4):
            lhs = jnp.concatenate([abuf[zs, y, pl.ds(base, BS), :] for y in range(2)], axis=1)
            tags = [
                abuf[zs, y, pl.ds(A_DATA + m * 2 + s, 1), :] for y in range(2) for s in range(2)
            ]
            sides = []
            for p in range(2):
                got, ids = [], []
                for t in (2 * p, 2 * p + 1):
                    n = jnp.maximum(wanted[t], 0)
                    got.append(bbuf[zs // 2, zs % 2, pl.ds(n * 4, 4)].reshape(BS, LANES))
                    tag = jnp.where(column == wanted[t], bbuf[zs // 2, zs % 2, B_DATA], 0.0)
                    ids.append(jnp.sum(tag, axis=0, keepdims=True))
                straight = jnp.where(left, got[0], got[1])
                crossed = pltpu.roll(jnp.where(left, got[1], got[0]), BS, 1)
                tag_straight = jnp.where(left, ids[0], ids[1])
                tag_crossed = pltpu.roll(jnp.where(left, ids[1], ids[0]), BS, 1)
                sides.append(jnp.concatenate([
                    jnp.where(t == tag_straight, straight, jnp.where(t == tag_crossed, crossed, 0.0))
                    for t in tags
                ], axis=0))
            rhs = jnp.concatenate(sides, axis=1)
            l_hi = lhs.astype(jnp.bfloat16)
            l_lo = (lhs - l_hi.astype(jnp.float32)).astype(jnp.bfloat16)
            r_hi = rhs.astype(jnp.bfloat16)
            r_lo = (rhs - r_hi.astype(jnp.float32)).astype(jnp.bfloat16)
            for l, r in ((l_hi, r_lo), (l_lo, r_hi), (l_hi, r_hi)):
                total += jnp.dot(l, r, preferred_element_type=jnp.float32)
        out = pl.multiple_of(m * LANES, LANES)
        for p in range(2):
            v0 = total[:32, p * LANES : (p + 1) * LANES]
            v1 = total[32:, p * LANES : (p + 1) * LANES]
            low, high = halves(v0, v1, left)
            pbuf[pl.ds(out + 2 * p, 32, stride=4), :] = low
            pbuf[pl.ds(out + 2 * p + 1, 32, stride=4), :] = high
        c_copy(m).start()
        return carry

    lax.fori_loop(0, ROWS, one_row, 0)

    for m in range(ROWS):
        c_copy(m).wait_recv()
        rows = pl.ds(m * LANES, LANES)
        o_ref[rows, :] = pbuf[rows, :] + rbuf[rows, :]
    for m in range(ROWS):
        c_copy(m).wait_send()

    @pl.when(a_even)
    def _():
        for c in a_own + a_swapped + even[0] + even[1]:
            c.wait_send()

    @pl.when(jnp.logical_not(a_even))
    def _():
        for c in odd[0] + odd[1] + odd_far[0] + odd_far[1]:
            c.wait_send()

    @pl.when(b_even)
    def _():
        for c in b_own + b_swapped:
            c.wait_send()

    @pl.when(jnp.logical_not(b_even))
    def _():
        for c in b_far[0] + b_far[1]:
            c.wait_send()


def interleaved(blocks):
    r, s, _ = blocks.shape
    return blocks.reshape(r, s, 32, LANES).transpose(0, 2, 1, 3).reshape(r * 32 * s, LANES)


def per_device(a_blocks, a_index, b_blocks, b_index, c_index):
    vmem = pl.BlockSpec(memory_space=pltpu.VMEM)
    smem = pl.BlockSpec(memory_space=pltpu.SMEM)
    out = pl.pallas_call(
        kernel,
        out_shape=jax.ShapeDtypeStruct((ROWS * LANES, LANES), jnp.float32),
        in_specs=[vmem, smem, vmem, smem, smem],
        out_specs=vmem,
        scratch_shapes=[
            pltpu.VMEM((4, 2, A_CHUNK, LANES), jnp.float32),
            pltpu.VMEM((2, 2, B_CHUNK, COLS, LANES), jnp.float32),
            pltpu.VMEM((ROWS * LANES, LANES), jnp.float32),
            pltpu.VMEM((ROWS * LANES, LANES), jnp.float32),
            pltpu.SemaphoreType.DMA((9,)),
            pltpu.SemaphoreType.DMA((4, 2, 2)),
            pltpu.SemaphoreType.DMA((5,)),
            pltpu.SemaphoreType.DMA((2, 2, 2)),
            pltpu.SemaphoreType.DMA((ROWS,)),
            pltpu.SemaphoreType.DMA((ROWS,)),
        ],
        compiler_params=pltpu.CompilerParams(
            collective_id=0, has_side_effects=True, vmem_limit_bytes=32 << 20
        ),
    )(interleaved(a_blocks), a_index, interleaved(b_blocks), b_index, c_index)
    return out.reshape(ROWS, 32, 4, LANES).transpose(0, 2, 1, 3).reshape(ROWS, 4, BS * BS)


def solution(mesh):
    placed = (
        P("row", "col", None),
        P("row", "col"),
        P("col", "row", None),
        P("col", "row"),
        P("row", "col"),
    )
    return jax.shard_map(
        per_device, mesh=mesh, in_specs=placed, out_specs=P("row", "col", None), check_vma=False
    )
```

```python
import jax
import jax.numpy as jnp
from jax import lax
from jax.experimental import pallas as pl
from jax.experimental.pallas import tpu as pltpu
from jax.sharding import PartitionSpec as P

BS = 64
LANES = 128
ROWS = 8
MINE = 4
COLS = 16
A_DATA = MINE * BS
A_PIECE = A_DATA + MINE * 2
GROUP = 16
B_HALF = COLS // 2 * 4 + 1
B_PARTS = ((0, 17), (17, 16))
TAGS = (0, 2 * B_HALF - 1)
X, Z = 4, 8
MESH = pl.DeviceIdType.MESH


def halves(x0, x1, left):
    return (
        jnp.where(left, x0, pltpu.roll(x1, BS, 1)),
        jnp.where(left, pltpu.roll(x0, BS, 1), x1),
    )


def kernel(
    a_hbm, ai_ref, b_hbm, bi_ref, ci_ref, o_ref,
    a_own, b_own, abuf, bbuf, total,
    isem, asend, arecv, bsend, brecv, fsend, frecv, csend, crecv,
):
    d = lax.axis_index("depth")
    row = lax.axis_index("row")
    col = lax.axis_index("col")
    x, yl = row % X, row // X
    z, yh = col // 2, col % 2
    way = 1 - 2 * d

    def z_at(k):
        return (z + Z - k * way) % Z

    def x_at(k):
        return (x + X - k * way) % X

    next_z = {"depth": d, "row": row, "col": z_at(-1) * 2 + yh}
    last_z = {"depth": d, "row": row, "col": z_at(1) * 2 + yh}
    next_x = {"depth": d, "row": yl * X + x_at(-1), "col": col}
    last_x = {"depth": d, "row": yl * X + x_at(1), "col": col}
    yh_peer = {"depth": d, "row": row, "col": z * 2 + (1 - yh)}
    yl_peer = {"depth": d, "row": (1 - yl) * X + x, "col": col}
    core_peer = {"depth": 1 - d, "row": row, "col": col}

    barrier = pltpu.get_barrier_semaphore()
    for peer in (next_z, last_z, next_x, last_x, yh_peer, yl_peer, core_peer):
        pl.semaphore_signal(barrier, inc=1, device_id=peer, device_id_type=MESH)

    mine_rows = pl.ds(pl.multiple_of(d * A_DATA, A_DATA), A_DATA)
    fetch_a = pltpu.make_async_copy(a_hbm.at[mine_rows, :], a_own, isem.at[0])
    fetch_b = pltpu.make_async_copy(b_hbm, b_own, isem.at[1])
    fetch_a.start()
    fetch_b.start()
    left = lax.broadcasted_iota(jnp.int32, (1, LANES), 1) < BS
    total[...] = jnp.zeros_like(total)

    fetch_a.wait()
    for m in range(MINE):
        x0 = a_own[pl.ds(m * BS, 32, stride=2), :]
        x1 = a_own[pl.ds(m * BS + 1, 32, stride=2), :]
        low, high = halves(x0, x1, left)
        abuf[z, yh, m * BS : m * BS + 32, :] = low
        abuf[z, yh, m * BS + 32 : m * BS + 64, :] = high
        for s in range(2):
            v = jnp.full((1, LANES), ai_ref[s, d * MINE + m])
            v = jnp.where(v < 0, -1, v + 1).astype(jnp.float32)
            r = A_DATA + m * 2 + s
            abuf[z, yh, r : r + 1, :] = v
    fetch_b.wait()
    for n in range(COLS):
        x0 = b_own[pl.ds(n * BS, 32, stride=2), :]
        x1 = b_own[pl.ds(n * BS + 1, 32, stride=2), :]
        low, high = halves(x0, x1, left)
        for g in range(4):
            group = 1 + n * 4 + g
            bbuf[row, group, pl.ds(0, 8, stride=2), :] = low[g * 8 : g * 8 + 8]
            bbuf[row, group, pl.ds(1, 8, stride=2), :] = high[g * 8 : g * 8 + 8]
        v0 = jnp.full((1, LANES), bi_ref[0, n])
        v1 = jnp.full((1, LANES), bi_ref[1, n])
        v = (jnp.where(left, v0, v1) + 1).astype(jnp.float32)
        r = n % 8
        bbuf[row, TAGS[n // 8], r : r + 1, :] = v

    pl.semaphore_wait(barrier, 7)

    a_y = (yh, 1 - yh)
    b_y = (yl, 1 - yl)

    def remote(view, to, send, recv):
        return pltpu.make_async_remote_copy(
            src_ref=view, dst_ref=view, send_sem=send, recv_sem=recv,
            device_id=to, device_id_type=MESH,
        )

    started = []

    def start(copy):
        copy.start()
        started.append(copy)

    def a_view(k, sub):
        return abuf.at[z_at(k), a_y[sub]]

    def b_view(k, sub, half, part):
        first, size = B_PARTS[part]
        return bbuf.at[b_y[sub] * X + x_at(k), pl.ds(half * B_HALF + first, size)]

    def a_next(k, sub):
        start(remote(a_view(k, sub), next_z, asend.at[k, sub], arecv.at[k + 1, sub]))

    def a_swap():
        start(remote(a_view(0, 0), yh_peer, asend.at[Z - 1, 0], arecv.at[0, 1]))

    def a_wait(k, sub):
        remote(a_view(k, sub), next_z, asend.at[0, 0], arecv.at[k, sub]).wait_recv()

    def b_next(k, sub, part):
        start(remote(b_view(k, sub, d, part), next_x, bsend.at[k, sub, part], brecv.at[k + 1, sub, part]))

    def b_swap(k, part):
        start(remote(b_view(k, 0, d, part), yl_peer, bsend.at[X + k, 0, part], brecv.at[k, 1, part]))

    def b_wait(k, sub, part):
        remote(b_view(k, sub, d, part), next_x, bsend.at[0, 0, 0], brecv.at[k, sub, part]).wait_recv()

    def b_share(k, sub, part):
        chunk = b_y[sub] * X + x_at(k)
        start(remote(b_view(k, sub, d, part), core_peer, fsend.at[chunk, part], frecv.at[chunk, part]))

    def b_shared(k, sub, part):
        chunk = b_y[sub] * X + x_at(k)
        view = b_view(k, sub, 1 - d, part)
        remote(view, core_peer, fsend.at[chunk, part], frecv.at[chunk, part]).wait_recv()

    def a_step(k, sub):
        a_wait(k, sub)
        a_next(k, sub)

    def b_step(k, sub, part):
        b_wait(k, sub, part)
        if (k, sub) in ((0, 1), (1, 0), (2, 0), (1, 1)):
            b_next(k, sub, part)
        if (k, sub) == (3, 0):
            b_swap(3, part)
        b_share(k, sub, part)

    column = lax.broadcasted_iota(jnp.int32, (8, LANES), 0)

    def tile(k, m):
        zs = z_at(k)
        base = m * BS
        if not isinstance(m, int):
            base = pl.multiple_of(base, BS)
        wanted = [ci_ref[t, d * MINE + m] for t in range(4)]
        lhs = jnp.concatenate([abuf[zs, y, pl.ds(base, BS), :] for y in range(2)], axis=1)
        tags = [abuf[zs, y, pl.ds(A_DATA + m * 2 + s, 1), :] for y in range(2) for s in range(2)]
        sides = []
        for p in range(2):
            got, ids = [], []
            for t in (2 * p, 2 * p + 1):
                n = jnp.maximum(wanted[t], 0)
                got.append(bbuf[zs, pl.ds(n * 4 + 1, 4)].reshape(BS, LANES))
                tag = jnp.where(column == wanted[t], bbuf[zs, TAGS[0], 0:8, :], 0.0)
                tag += jnp.where(column + 8 == wanted[t], bbuf[zs, TAGS[1], 0:8, :], 0.0)
                ids.append(jnp.sum(tag, axis=0, keepdims=True))
            straight = jnp.where(left, got[0], got[1])
            crossed = pltpu.roll(jnp.where(left, got[1], got[0]), BS, 1)
            tag_straight = jnp.where(left, ids[0], ids[1])
            tag_crossed = pltpu.roll(jnp.where(left, ids[1], ids[0]), BS, 1)
            sides.append(jnp.concatenate([
                jnp.where(t == tag_straight, straight, jnp.where(t == tag_crossed, crossed, 0.0))
                for t in tags
            ], axis=0))
        rhs = jnp.concatenate(sides, axis=1)
        l_hi = lhs.astype(jnp.bfloat16)
        l_lo = (lhs - l_hi.astype(jnp.float32)).astype(jnp.bfloat16)
        r_hi = rhs.astype(jnp.bfloat16)
        r_lo = (rhs - r_hi.astype(jnp.float32)).astype(jnp.bfloat16)
        new = total[m]
        for l, r in ((l_hi, r_lo), (l_lo, r_hi), (l_hi, r_hi)):
            new += jnp.dot(l, r, preferred_element_type=jnp.float32)
        return new

    def tiles(first, last):
        def body(i, carry):
            k, m = i // MINE, i % MINE
            total[m] = tile(k, m)
            return carry

        lax.fori_loop(first * MINE, last * MINE, body, 0)

    a_swap()
    a_next(0, 0)
    for part in range(2):
        b_next(0, 0, part)
    a_step(1, 0)
    b_step(1, 0, 0)
    a_step(0, 1)
    for part in range(2):
        b_swap(0, part)
    b_step(1, 0, 1)
    a_step(2, 0)
    b_step(2, 0, 0)
    a_step(1, 1)
    b_step(2, 0, 1)
    a_step(3, 0)
    b_step(3, 0, 0)
    a_step(2, 1)
    b_step(3, 0, 1)
    a_step(4, 0)
    b_step(0, 1, 0)
    a_step(3, 1)
    b_step(0, 1, 1)
    a_step(5, 0)
    b_step(1, 1, 0)
    a_step(4, 1)
    b_step(1, 1, 1)
    b_step(3, 1, 0)
    b_step(3, 1, 1)
    a_step(6, 0)
    b_step(2, 1, 0)
    a_step(5, 1)
    b_step(2, 1, 1)
    for k in range(X):
        for sub in range(2):
            if (k, sub) != (0, 0):
                for part in range(2):
                    b_shared(k, sub, part)
    tiles(0, 2)
    a_step(6, 1)
    tiles(2, 7)
    a_wait(7, 0)
    a_wait(7, 1)

    def c_copy(m):
        at = pl.ds(pl.multiple_of((d * MINE + m) * LANES, LANES), LANES)
        return remote(o_ref.at[at, :], core_peer, csend.at[m], crecv.at[m])

    def last(m, carry):
        done = tile(7, m)
        out = pl.multiple_of((d * MINE + m) * LANES, LANES)
        for p in range(2):
            v0 = done[:32, p * LANES : (p + 1) * LANES]
            v1 = done[32:, p * LANES : (p + 1) * LANES]
            low, high = halves(v0, v1, left)
            o_ref[pl.ds(out + 2 * p, 32, stride=4), :] = low
            o_ref[pl.ds(out + 2 * p + 1, 32, stride=4), :] = high
        c_copy(m).start()
        return carry

    lax.fori_loop(0, MINE, last, 0)

    for copy in started:
        copy.wait_send()
    for m in range(MINE):
        at = pl.ds(pl.multiple_of(((1 - d) * MINE + m) * LANES, LANES), LANES)
        remote(o_ref.at[at, :], core_peer, csend.at[m], crecv.at[m]).wait_recv()
        c_copy(m).wait_send()


def interleaved(blocks):
    r, s, _ = blocks.shape
    return blocks.reshape(r, s, 32, LANES).transpose(0, 2, 1, 3).reshape(r * 32 * s, LANES)


def per_device(a_blocks, a_index, b_blocks, b_index, c_index):
    vmem = pl.BlockSpec(memory_space=pltpu.VMEM)
    smem = pl.BlockSpec(memory_space=pltpu.SMEM)
    hbm = pl.BlockSpec(memory_space=pltpu.HBM)
    dma = pltpu.SemaphoreType.DMA
    out = pl.pallas_call(
        kernel,
        out_shape=jax.ShapeDtypeStruct((ROWS * LANES, LANES), jnp.float32),
        in_specs=[hbm, smem, hbm, smem, smem],
        out_specs=vmem,
        scratch_shapes=[
            pltpu.VMEM((A_DATA, LANES), jnp.float32),
            pltpu.VMEM((COLS * BS, LANES), jnp.float32),
            pltpu.VMEM((Z, 2, A_PIECE, LANES), jnp.float32),
            pltpu.VMEM((2 * X, 2 * B_HALF, GROUP, LANES), jnp.float32),
            pltpu.VMEM((MINE, BS, 4 * BS), jnp.float32),
            dma((2,)),
            dma((Z, 2)),
            dma((Z, 2)),
            dma((2 * X, 2, 2)),
            dma((X, 2, 2)),
            dma((2 * X, 2)),
            dma((2 * X, 2)),
            dma((MINE,)),
            dma((MINE,)),
        ],
        compiler_params=pltpu.CompilerParams(
            collective_id=0, has_side_effects=True, vmem_limit_bytes=56 << 20
        ),
    )(interleaved(a_blocks), a_index.T, interleaved(b_blocks), b_index.T, c_index.T)
    return out.reshape(ROWS, 32, 4, LANES).transpose(0, 2, 1, 3).reshape(ROWS, 4, BS * BS)


def solution(mesh):
    placed = (
        P("row", "col", None),
        P("row", "col"),
        P("col", "row", None),
        P("col", "row"),
        P("row", "col"),
    )
    return jax.shard_map(
        per_device, mesh=mesh, in_specs=placed, out_specs=P("row", "col", None), check_vma=False
    )
```

```python
import jax
import jax.numpy as jnp
from jax import lax
from jax.experimental import pallas as pl
from jax.experimental.pallas import tpu as pltpu
from jax.sharding import PartitionSpec as P

BS = 64
LANES = 128
ROWS = 8
MINE = 4
COLS = 16
A_DATA = MINE * BS
A_PIECE = A_DATA + MINE * 2
GROUP = 16
B_HALF = COLS // 2 * 4 + 1
B_PARTS = ((0, 17), (17, 16))
A_PARTS = ((0, 136), (136, 128))
TAGS = (0, 2 * B_HALF - 1)
X, Z = 4, 8
WAYS = (1, -1)
MESH = pl.DeviceIdType.MESH


def halves(x0, x1, left):
    return (
        jnp.where(left, x0, pltpu.roll(x1, BS, 1)),
        jnp.where(left, pltpu.roll(x0, BS, 1), x1),
    )


def kernel(
    a_hbm, ai_ref, b_hbm, bi_ref, ci_ref, o_ref,
    a_own, b_own, abuf, bbuf, total,
    isem, asend, arecv, bsend, brecv, fsend, frecv, csend, crecv,
):
    d = lax.axis_index("depth")
    row = lax.axis_index("row")
    col = lax.axis_index("col")
    x, yl = row % X, row // X
    z, yh = col // 2, col % 2

    def z_at(k):
        return (z + k + Z) % Z

    def x_at(k):
        return (x + k + X) % X

    to_z = [{"depth": d, "row": row, "col": z_at(w) * 2 + yh} for w in WAYS]
    to_x = [{"depth": d, "row": yl * X + x_at(w), "col": col} for w in WAYS]
    yh_peer = {"depth": d, "row": row, "col": z * 2 + (1 - yh)}
    yl_peer = {"depth": d, "row": (1 - yl) * X + x, "col": col}
    core_peer = {"depth": 1 - d, "row": row, "col": col}

    barrier = pltpu.get_barrier_semaphore()
    for peer in (*to_z, *to_x, yh_peer, yl_peer, core_peer):
        pl.semaphore_signal(barrier, inc=1, device_id=peer, device_id_type=MESH)

    mine_rows = pl.ds(pl.multiple_of(d * A_DATA, A_DATA), A_DATA)
    fetch_a = pltpu.make_async_copy(a_hbm.at[mine_rows, :], a_own, isem.at[0])
    fetch_b = pltpu.make_async_copy(b_hbm, b_own, isem.at[1])
    fetch_a.start()
    fetch_b.start()
    left = lax.broadcasted_iota(jnp.int32, (1, LANES), 1) < BS
    total[...] = jnp.zeros_like(total)

    fetch_a.wait()
    for m in range(MINE):
        x0 = a_own[pl.ds(m * BS, 32, stride=2), :]
        x1 = a_own[pl.ds(m * BS + 1, 32, stride=2), :]
        low, high = halves(x0, x1, left)
        abuf[z, yh, m * BS : m * BS + 32, :] = low
        abuf[z, yh, m * BS + 32 : m * BS + 64, :] = high
        for s in range(2):
            v = jnp.full((1, LANES), ai_ref[s, d * MINE + m])
            v = jnp.where(v < 0, -1, v + 1).astype(jnp.float32)
            r = A_DATA + m * 2 + s
            abuf[z, yh, r : r + 1, :] = v
    fetch_b.wait()
    for n in range(COLS):
        x0 = b_own[pl.ds(n * BS, 32, stride=2), :]
        x1 = b_own[pl.ds(n * BS + 1, 32, stride=2), :]
        low, high = halves(x0, x1, left)
        for g in range(4):
            group = 1 + n * 4 + g
            bbuf[row, group, pl.ds(0, 8, stride=2), :] = low[g * 8 : g * 8 + 8]
            bbuf[row, group, pl.ds(1, 8, stride=2), :] = high[g * 8 : g * 8 + 8]
        v0 = jnp.full((1, LANES), bi_ref[0, n])
        v1 = jnp.full((1, LANES), bi_ref[1, n])
        v = (jnp.where(left, v0, v1) + 1).astype(jnp.float32)
        r = n % 8
        bbuf[row, TAGS[n // 8], r : r + 1, :] = v

    pl.semaphore_wait(barrier, 7)

    a_y = (yh, 1 - yh)
    b_y = (yl, 1 - yl)

    def remote(view, to, send, recv):
        return pltpu.make_async_remote_copy(
            src_ref=view, dst_ref=view, send_sem=send, recv_sem=recv,
            device_id=to, device_id_type=MESH,
        )

    started = []

    def start(copy):
        copy.start()
        started.append(copy)

    def a_view(e, k, sub, part=None):
        ref = abuf.at[z_at(-WAYS[e] * k), a_y[sub]]
        return ref if part is None else ref.at[pl.ds(*A_PARTS[part]), :]

    def a_next(e, k, sub, part=None):
        view = a_view(e, k, sub, part)
        start(remote(view, to_z[e], asend.at[e, k, sub], arecv.at[e, k + 1, sub]))

    def a_swap():
        start(remote(a_view(0, 0, 0), yh_peer, asend.at[0, 4, 0], arecv.at[0, 0, 1]))

    def a_wait(e, k, sub, part=None):
        remote(a_view(e, k, sub, part), to_z[e], asend.at[e, 0, 0], arecv.at[e, k, sub]).wait_recv()

    def a_step(k, sub):
        for e in range(2):
            a_wait(e, k, sub)
            a_next(e, k, sub, e if k == 3 else None)

    def a_last(sub):
        for e in range(2):
            a_wait(e, 4, sub, e)

    def a_other():
        a_wait(0, 0, 1)
        for e in range(2):
            a_next(e, 0, 1)

    def b_view(chunk, half, part):
        first, size = B_PARTS[part]
        return bbuf.at[chunk, pl.ds(half * B_HALF + first, size)]

    def b_chunk(e, k, sub):
        return b_y[sub] * X + x_at(-WAYS[e] * k)

    def b_next(e, k, sub, part):
        view = b_view(b_chunk(e, k, sub), d, part)
        start(remote(view, to_x[e], bsend.at[e, k, sub, part], brecv.at[e, k + 1, sub, part]))

    def b_swap(part):
        view = b_view(b_chunk(0, 0, 0), d, part)
        start(remote(view, yl_peer, bsend.at[0, 2, 0, part], brecv.at[0, 0, 1, part]))

    def b_take(e, k, sub, part):
        chunk = b_chunk(e, k, sub)
        view = b_view(chunk, d, part)
        remote(view, to_x[e], bsend.at[e, 0, 0, part], brecv.at[e, k, sub, part]).wait_recv()
        start(remote(view, core_peer, fsend.at[chunk, part], frecv.at[chunk, part]))

    def b_step(sub):
        for i in range(2):
            for e in range(2):
                part = e if i == 0 else 1 - e
                b_take(e, 1, sub, part)
                if i == 0:
                    b_next(e, 1, sub, part)

    def b_other(part):
        b_take(0, 0, 1, part)
        for e in range(2):
            b_next(e, 0, 1, part)

    def b_last(sub):
        for e in range(2):
            b_take(e, 2, sub, e)

    def b_shared():
        for k in range(X):
            for sub in range(2):
                if (k, sub) != (0, 0):
                    chunk = b_chunk(0, k, sub)
                    for part in range(2):
                        view = b_view(chunk, 1 - d, part)
                        remote(view, core_peer, fsend.at[chunk, part], frecv.at[chunk, part]).wait_recv()

    column = lax.broadcasted_iota(jnp.int32, (8, LANES), 0)

    def tile(new, k, m):
        zs = z_at(k)
        base = pl.multiple_of(m * BS, BS)
        wanted = [ci_ref[t, d * MINE + m] for t in range(4)]
        lhs = jnp.concatenate([abuf[zs, y, pl.ds(base, BS), :] for y in range(2)], axis=1)
        tags = [abuf[zs, y, pl.ds(A_DATA + m * 2 + s, 1), :] for y in range(2) for s in range(2)]
        sides = []
        for p in range(2):
            got, ids = [], []
            for t in (2 * p, 2 * p + 1):
                n = jnp.maximum(wanted[t], 0)
                got.append(bbuf[zs, pl.ds(n * 4 + 1, 4)].reshape(BS, LANES))
                tag = jnp.where(column == wanted[t], bbuf[zs, TAGS[0], 0:8, :], 0.0)
                tag += jnp.where(column + 8 == wanted[t], bbuf[zs, TAGS[1], 0:8, :], 0.0)
                ids.append(jnp.sum(tag, axis=0, keepdims=True))
            straight = jnp.where(left, got[0], got[1])
            crossed = pltpu.roll(jnp.where(left, got[1], got[0]), BS, 1)
            tag_straight = jnp.where(left, ids[0], ids[1])
            tag_crossed = pltpu.roll(jnp.where(left, ids[1], ids[0]), BS, 1)
            sides.append(jnp.concatenate([
                jnp.where(t == tag_straight, straight, jnp.where(t == tag_crossed, crossed, 0.0))
                for t in tags
            ], axis=0))
        rhs = jnp.concatenate(sides, axis=1)
        l_hi = lhs.astype(jnp.bfloat16)
        l_lo = (lhs - l_hi.astype(jnp.float32)).astype(jnp.bfloat16)
        r_hi = rhs.astype(jnp.bfloat16)
        r_lo = (rhs - r_hi.astype(jnp.float32)).astype(jnp.bfloat16)
        for l, r in ((l_hi, r_lo), (l_lo, r_hi), (l_hi, r_hi)):
            new += jnp.dot(l, r, preferred_element_type=jnp.float32)
        return new

    def summed(m, panels):
        new = total[m]
        for k in panels:
            new = tile(new, k, m)
        return new

    def tiles(*panels):
        def body(m, carry):
            total[m] = summed(m, panels)
            return carry

        lax.fori_loop(0, MINE, body, 0)

    a_swap()
    for e in range(2):
        a_next(e, 0, 0)
    for i in range(2):
        for e in range(2):
            b_next(e, 0, 0, e if i == 0 else 1 - e)
    for part in range(2):
        b_swap(part)
    a_step(1, 0)
    b_step(0)
    a_other()
    b_other(0)
    a_step(2, 0)
    b_other(1)
    a_step(1, 1)
    b_last(0)
    a_step(3, 0)
    a_step(2, 1)
    b_step(1)
    a_last(0)
    b_last(1)
    a_step(3, 1)
    b_shared()
    tiles(0, 1, -1, 2, -2)
    a_last(1)

    def c_copy(m):
        at = pl.ds(pl.multiple_of((d * MINE + m) * LANES, LANES), LANES)
        return remote(o_ref.at[at, :], core_peer, csend.at[m], crecv.at[m])

    def last(m, carry):
        done = summed(m, (3, -3, 4))
        out = pl.multiple_of((d * MINE + m) * LANES, LANES)
        for p in range(2):
            v0 = done[:32, p * LANES : (p + 1) * LANES]
            v1 = done[32:, p * LANES : (p + 1) * LANES]
            low, high = halves(v0, v1, left)
            o_ref[pl.ds(out + 2 * p, 32, stride=4), :] = low
            o_ref[pl.ds(out + 2 * p + 1, 32, stride=4), :] = high
        c_copy(m).start()
        return carry

    lax.fori_loop(0, MINE, last, 0)

    for copy in started:
        copy.wait_send()
    for m in range(MINE):
        at = pl.ds(pl.multiple_of(((1 - d) * MINE + m) * LANES, LANES), LANES)
        remote(o_ref.at[at, :], core_peer, csend.at[m], crecv.at[m]).wait_recv()
        c_copy(m).wait_send()


def interleaved(blocks):
    r, s, _ = blocks.shape
    return blocks.reshape(r, s, 32, LANES).transpose(0, 2, 1, 3).reshape(r * 32 * s, LANES)


def per_device(a_blocks, a_index, b_blocks, b_index, c_index):
    vmem = pl.BlockSpec(memory_space=pltpu.VMEM)
    smem = pl.BlockSpec(memory_space=pltpu.SMEM)
    hbm = pl.BlockSpec(memory_space=pltpu.HBM)
    dma = pltpu.SemaphoreType.DMA
    out = pl.pallas_call(
        kernel,
        out_shape=jax.ShapeDtypeStruct((ROWS * LANES, LANES), jnp.float32),
        in_specs=[hbm, smem, hbm, smem, smem],
        out_specs=vmem,
        scratch_shapes=[
            pltpu.VMEM((A_DATA, LANES), jnp.float32),
            pltpu.VMEM((COLS * BS, LANES), jnp.float32),
            pltpu.VMEM((Z, 2, A_PIECE, LANES), jnp.float32),
            pltpu.VMEM((2 * X, 2 * B_HALF, GROUP, LANES), jnp.float32),
            pltpu.VMEM((MINE, BS, 4 * BS), jnp.float32),
            dma((2,)),
            dma((2, 5, 2)),
            dma((2, 5, 2)),
            dma((2, 3, 2, 2)),
            dma((2, 3, 2, 2)),
            dma((2 * X, 2)),
            dma((2 * X, 2)),
            dma((MINE,)),
            dma((MINE,)),
        ],
        compiler_params=pltpu.CompilerParams(
            collective_id=0, has_side_effects=True, vmem_limit_bytes=56 << 20
        ),
    )(interleaved(a_blocks), a_index.T, interleaved(b_blocks), b_index.T, c_index.T)
    return out.reshape(ROWS, 32, 4, LANES).transpose(0, 2, 1, 3).reshape(ROWS, 4, BS * BS)


def solution(mesh):
    placed = (
        P("row", "col", None),
        P("row", "col"),
        P("col", "row", None),
        P("col", "row"),
        P("row", "col"),
    )
    return jax.shard_map(
        per_device, mesh=mesh, in_specs=placed, out_specs=P("row", "col", None), check_vma=False
    )
```

```python
import jax
import jax.numpy as jnp
from jax import lax
from jax.experimental import pallas as pl
from jax.experimental.pallas import tpu as pltpu
from jax.sharding import PartitionSpec as P

BS = 64
LANES = 128
ROWS = 8
MINE = 4
COLS = 16
A_DATA = MINE * BS
A_PIECE = A_DATA + MINE * 2
GROUP = 16
B_HALF = COLS // 2 * 4 + 1
B_PARTS = ((0, 17), (17, 16))
A_PARTS = ((0, 136), (136, 128))
TAGS = (0, 2 * B_HALF - 1)
X, Z = 4, 8
WAYS = (1, -1)
MESH = pl.DeviceIdType.MESH


def halves(x0, x1, left):
    return (
        jnp.where(left, x0, pltpu.roll(x1, BS, 1)),
        jnp.where(left, pltpu.roll(x0, BS, 1), x1),
    )


def kernel(
    a_hbm, ai_hbm, b_hbm, bi_hbm, ci_hbm, o_ref,
    ai_ref, bi_ref, ci_ref, a_own, b_own, abuf, bbuf, total,
    isem, asend, arecv, bsend, brecv, fsend, frecv, csend, crecv,
):
    d = lax.axis_index("depth")
    row = lax.axis_index("row")
    col = lax.axis_index("col")
    x, yl = row % X, row // X
    z, yh = col // 2, col % 2

    def z_at(k):
        return (z + k + Z) % Z

    def x_at(k):
        return (x + k + X) % X

    to_z = [{"depth": d, "row": row, "col": z_at(w) * 2 + yh} for w in WAYS]
    to_x = [{"depth": d, "row": yl * X + x_at(w), "col": col} for w in WAYS]
    to_zy = [{"depth": d, "row": row, "col": z_at(w) * 2 + (1 - yh)} for w in WAYS]
    yh_peer = {"depth": d, "row": row, "col": z * 2 + (1 - yh)}
    yl_peer = {"depth": d, "row": (1 - yl) * X + x, "col": col}
    core_peer = {"depth": 1 - d, "row": row, "col": col}

    barrier = pltpu.get_barrier_semaphore()
    for peer in (*to_z, *to_x, yh_peer, yl_peer, core_peer):
        pl.semaphore_signal(barrier, inc=1, device_id=peer, device_id_type=MESH)

    mine_rows = pl.ds(pl.multiple_of(d * A_DATA, A_DATA), A_DATA)
    fetch_a = pltpu.make_async_copy(a_hbm.at[mine_rows, :], a_own, isem.at[0])
    fetch_b = pltpu.make_async_copy(b_hbm, b_own, isem.at[1])
    fetch_a.start()
    fetch_ai = pltpu.make_async_copy(ai_hbm, ai_ref, isem.at[2])
    fetch_bi = pltpu.make_async_copy(bi_hbm, bi_ref, isem.at[3])
    fetch_ci = pltpu.make_async_copy(ci_hbm, ci_ref, isem.at[4])
    fetch_ai.start()
    fetch_b.start()
    fetch_bi.start()
    fetch_ci.start()
    left = lax.broadcasted_iota(jnp.int32, (1, LANES), 1) < BS
    total[...] = jnp.zeros_like(total)

    fetch_a.wait()
    fetch_ai.wait()
    for m in range(MINE):
        x0 = a_own[pl.ds(m * BS, 32, stride=2), :]
        x1 = a_own[pl.ds(m * BS + 1, 32, stride=2), :]
        low, high = halves(x0, x1, left)
        abuf[z, yh, m * BS : m * BS + 32, :] = low
        abuf[z, yh, m * BS + 32 : m * BS + 64, :] = high
        for s in range(2):
            v = jnp.full((1, LANES), ai_ref[s, d * MINE + m])
            v = jnp.where(v < 0, -1, v + 1).astype(jnp.float32)
            r = A_DATA + m * 2 + s
            abuf[z, yh, r : r + 1, :] = v
    pl.semaphore_wait(barrier, 7)

    a_y = (yh, 1 - yh)
    b_y = (yl, 1 - yl)

    def remote(view, to, send, recv):
        return pltpu.make_async_remote_copy(
            src_ref=view, dst_ref=view, send_sem=send, recv_sem=recv,
            device_id=to, device_id_type=MESH,
        )

    started = []

    def start(copy):
        copy.start()
        started.append(copy)

    def a_view(e, k, sub, part):
        return abuf.at[z_at(-WAYS[e] * k), a_y[sub], pl.ds(*A_PARTS[part]), :]

    def a_next(e, k, sub, part):
        view = a_view(e, k, sub, part)
        start(remote(view, to_z[e], asend.at[e, k, sub, part], arecv.at[e, k + 1, sub, part]))

    def a_swap(part):
        view = a_view(0, 0, 0, part)
        start(remote(view, yh_peer, asend.at[0, 4, 0, part], arecv.at[0, 0, 1, part]))

    def a_across(e, part):
        view = a_view(0, 0, 0, part)
        start(remote(view, to_zy[e], asend.at[e, 0, 1, part], arecv.at[e, 1, 1, part]))

    def a_wait(e, k, sub, part):
        view = a_view(e, k, sub, part)
        remote(view, to_z[e], asend.at[e, 0, 0, 0], arecv.at[e, k, sub, part]).wait_recv()

    def a_over(e, k, part):
        view = a_view(e, k, 0, part)
        start(remote(view, yh_peer, asend.at[e, k, 1, part], arecv.at[e, k, 1, part]))

    def a_step(k, sub, i):
        for e in range(2):
            part = i if sub else (e + i) % 2
            a_wait(e, k, sub, part)
            if k + sub < 3 or (k == 3 and part == e):
                a_next(e, k, sub, part)
            if k == 3:
                a_over(e, k, part)

    def a_other(part):
        a_wait(0, 0, 1, part)
        for e in range(2):
            a_next(e, 0, 1, part)

    def a_last(sub):
        for e in range(2):
            a_wait(e, 4, sub, e)
            if sub == 0:
                a_over(e, 4, e)

    def a_far(k):
        for e in range(2):
            for part in range(2):
                a_wait(e, k, 1, part)

    def b_view(chunk, half, part):
        first, size = B_PARTS[part]
        return bbuf.at[chunk, pl.ds(half * B_HALF + first, size)]

    def b_chunk(e, k, sub):
        return b_y[sub] * X + x_at(-WAYS[e] * k)

    def b_next(e, k, sub, part):
        view = b_view(b_chunk(e, k, sub), d, part)
        start(remote(view, to_x[e], bsend.at[e, k, sub, part], brecv.at[e, k + 1, sub, part]))

    def b_swap(part):
        view = b_view(b_chunk(0, 0, 0), d, part)
        start(remote(view, yl_peer, bsend.at[0, 2, 0, part], brecv.at[0, 0, 1, part]))

    def b_take(e, k, sub, part):
        chunk = b_chunk(e, k, sub)
        view = b_view(chunk, d, part)
        remote(view, to_x[e], bsend.at[e, 0, 0, part], brecv.at[e, k, sub, part]).wait_recv()
        start(remote(view, core_peer, fsend.at[chunk, part], frecv.at[chunk, part]))

    def b_step(sub, i):
        for e in range(2):
            part = i if sub else (e + i) % 2
            b_take(e, 1, sub, part)
            if part == e:
                b_next(e, 1, sub, part)

    def b_other(part):
        b_take(0, 0, 1, part)
        for e in range(2):
            b_next(e, 0, 1, part)

    def b_last(sub):
        for e in range(2):
            b_take(e, 2, sub, e)

    def b_shared():
        for k in range(X):
            for sub in range(2):
                if (k, sub) != (0, 0):
                    chunk = b_chunk(0, k, sub)
                    for part in range(2):
                        view = b_view(chunk, 1 - d, part)
                        remote(view, core_peer, fsend.at[chunk, part], frecv.at[chunk, part]).wait_recv()

    column = lax.broadcasted_iota(jnp.int32, (8, LANES), 0)

    def tile(new, k, m):
        zs = z_at(k)
        base = pl.multiple_of(m * BS, BS)
        wanted = [ci_ref[t, d * MINE + m] for t in range(4)]
        lhs = jnp.concatenate([abuf[zs, y, pl.ds(base, BS), :] for y in range(2)], axis=1)
        tags = [abuf[zs, y, pl.ds(A_DATA + m * 2 + s, 1), :] for y in range(2) for s in range(2)]
        sides = []
        for p in range(2):
            got, ids = [], []
            for t in (2 * p, 2 * p + 1):
                n = jnp.maximum(wanted[t], 0)
                got.append(bbuf[zs, pl.ds(n * 4 + 1, 4)].reshape(BS, LANES))
                tag = jnp.where(column == wanted[t], bbuf[zs, TAGS[0], 0:8, :], 0.0)
                tag += jnp.where(column + 8 == wanted[t], bbuf[zs, TAGS[1], 0:8, :], 0.0)
                ids.append(jnp.sum(tag, axis=0, keepdims=True))
            straight = jnp.where(left, got[0], got[1])
            crossed = pltpu.roll(jnp.where(left, got[1], got[0]), BS, 1)
            tag_straight = jnp.where(left, ids[0], ids[1])
            tag_crossed = pltpu.roll(jnp.where(left, ids[1], ids[0]), BS, 1)
            sides.append(jnp.concatenate([
                jnp.where(t == tag_straight, straight, jnp.where(t == tag_crossed, crossed, 0.0))
                for t in tags
            ], axis=0))
        rhs = jnp.concatenate(sides, axis=1)
        l_hi = lhs.astype(jnp.bfloat16)
        l_lo = (lhs - l_hi.astype(jnp.float32)).astype(jnp.bfloat16)
        r_hi = rhs.astype(jnp.bfloat16)
        r_lo = (rhs - r_hi.astype(jnp.float32)).astype(jnp.bfloat16)
        for l, r in ((l_hi, r_lo), (l_lo, r_hi), (l_hi, r_hi)):
            new += jnp.dot(l, r, preferred_element_type=jnp.float32)
        return new

    def summed(m, panels):
        new = total[m]
        for k in panels:
            new = tile(new, k, m)
        return new

    def tiles(*panels):
        def body(m, carry):
            total[m] = summed(m, panels)
            return carry

        lax.fori_loop(0, MINE, body, 0)

    a_swap(0)
    for i in range(2):
        for e in range(2):
            a_next(e, 0, 0, (e + i) % 2)
    fetch_b.wait()
    fetch_bi.wait()
    fetch_ci.wait()
    for n in range(COLS):
        x0 = b_own[pl.ds(n * BS, 32, stride=2), :]
        x1 = b_own[pl.ds(n * BS + 1, 32, stride=2), :]
        low, high = halves(x0, x1, left)
        for g in range(4):
            group = 1 + n * 4 + g
            bbuf[row, group, pl.ds(0, 8, stride=2), :] = low[g * 8 : g * 8 + 8]
            bbuf[row, group, pl.ds(1, 8, stride=2), :] = high[g * 8 : g * 8 + 8]
        v0 = jnp.full((1, LANES), bi_ref[0, n])
        v1 = jnp.full((1, LANES), bi_ref[1, n])
        v = (jnp.where(left, v0, v1) + 1).astype(jnp.float32)
        r = n % 8
        bbuf[row, TAGS[n // 8], r : r + 1, :] = v

    b_swap(0)
    a_swap(1)
    b_swap(1)
    for i in range(2):
        for e in range(2):
            b_next(e, 0, 0, (e + i) % 2)
    a_step(1, 0, 0)
    a_other(0)
    a_step(1, 0, 1)
    b_step(0, 0)
    b_other(0)
    a_step(2, 0, 0)
    b_step(0, 1)
    a_other(1)
    b_other(1)
    a_step(2, 0, 1)
    a_step(1, 1, 0)
    b_last(0)
    a_step(3, 0, 0)
    a_step(1, 1, 1)
    a_step(3, 0, 1)
    b_step(1, 0)
    b_step(1, 1)
    a_last(0)
    b_last(1)
    a_far(2)
    b_shared()
    tiles(0, 1, -1, 2, -2)
    a_far(3)
    a_last(1)

    def c_copy(m):
        at = pl.ds(pl.multiple_of((d * MINE + m) * LANES, LANES), LANES)
        return remote(o_ref.at[at, :], core_peer, csend.at[m], crecv.at[m])

    def last(m, carry):
        done = summed(m, (3, -3, 4))
        out = pl.multiple_of((d * MINE + m) * LANES, LANES)
        for p in range(2):
            v0 = done[:32, p * LANES : (p + 1) * LANES]
            v1 = done[32:, p * LANES : (p + 1) * LANES]
            low, high = halves(v0, v1, left)
            o_ref[pl.ds(out + 2 * p, 32, stride=4), :] = low
            o_ref[pl.ds(out + 2 * p + 1, 32, stride=4), :] = high
        c_copy(m).start()
        return carry

    lax.fori_loop(0, MINE, last, 0)

    for copy in started:
        copy.wait_send()
    for m in range(MINE):
        at = pl.ds(pl.multiple_of(((1 - d) * MINE + m) * LANES, LANES), LANES)
        remote(o_ref.at[at, :], core_peer, csend.at[m], crecv.at[m]).wait_recv()
        c_copy(m).wait_send()


def interleaved(blocks):
    r, s, _ = blocks.shape
    return blocks.reshape(r, s, 32, LANES).transpose(0, 2, 1, 3).reshape(r * 32 * s, LANES)


def per_device(a_blocks, a_index, b_blocks, b_index, c_index):
    vmem = pl.BlockSpec(memory_space=pltpu.VMEM)
    hbm = pl.BlockSpec(memory_space=pltpu.HBM)
    dma = pltpu.SemaphoreType.DMA
    out = pl.pallas_call(
        kernel,
        out_shape=pltpu.VMEM((ROWS * LANES, LANES), jnp.float32),
        in_specs=[hbm] * 5,
        out_specs=vmem,
        scratch_shapes=[
            pltpu.SMEM((2, ROWS), jnp.int32),
            pltpu.SMEM((2, COLS), jnp.int32),
            pltpu.SMEM((4, ROWS), jnp.int32),
            pltpu.VMEM((A_DATA, LANES), jnp.float32),
            pltpu.VMEM((COLS * BS, LANES), jnp.float32),
            pltpu.VMEM((Z, 2, A_PIECE, LANES), jnp.float32),
            pltpu.VMEM((2 * X, 2 * B_HALF, GROUP, LANES), jnp.float32),
            pltpu.VMEM((MINE, BS, 4 * BS), jnp.float32),
            dma((5,)),
            dma((2, 5, 2, 2)),
            dma((2, 5, 2, 2)),
            dma((2, 3, 2, 2)),
            dma((2, 3, 2, 2)),
            dma((2 * X, 2)),
            dma((2 * X, 2)),
            dma((MINE,)),
            dma((MINE,)),
        ],
        compiler_params=pltpu.CompilerParams(
            collective_id=0, has_side_effects=True, vmem_limit_bytes=56 << 20
        ),
    )(interleaved(a_blocks), a_index.T, interleaved(b_blocks), b_index.T, c_index.T)
    return out.reshape(ROWS, 32, 4, LANES).transpose(0, 2, 1, 3).reshape(ROWS, 4, BS * BS)


def solution(mesh):
    placed = (
        P("row", "col", None),
        P("row", "col"),
        P("col", "row", None),
        P("col", "row"),
        P("row", "col"),
    )
    return jax.shard_map(
        per_device, mesh=mesh, in_specs=placed, out_specs=P("row", "col", None), check_vma=False
    )
```

```python
import jax
import jax.numpy as jnp
from jax import lax
from jax.experimental import pallas as pl
from jax.experimental.pallas import tpu as pltpu
from jax.sharding import PartitionSpec as P

BS = 64
LANES = 128
ROWS = 8
MINE = 4
COLS = 16
A_DATA = MINE * BS
A_PIECE = A_DATA + MINE * 2
GROUP = 8
B_HALF = COLS // 2 * 8 + 1
B_PARTS = ((0, 33), (33, 32))
A_PARTS = ((0, 136), (136, 128))
TAGS = (0, 2 * B_HALF - 1)
X, Z = 4, 8
WAYS = (1, -1)
MESH = pl.DeviceIdType.MESH


def halves(x0, x1, left):
    return (
        jnp.where(left, x0, pltpu.roll(x1, BS, 1)),
        jnp.where(left, pltpu.roll(x0, BS, 1), x1),
    )


def kernel(
    a_hbm, ai_hbm, b_hbm, bi_hbm, ci_hbm, o_ref,
    ai_ref, bi_ref, ci_ref, a_own, b_own, abuf, bbuf, total,
    isem, asend, arecv, bsend, brecv, fsend, frecv, csend, crecv,
):
    d = lax.axis_index("depth")
    row = lax.axis_index("row")
    col = lax.axis_index("col")
    x, yl = row % X, row // X
    z, yh = col // 2, col % 2

    def z_at(k):
        return (z + k + Z) % Z

    def x_at(k):
        return (x + k + X) % X

    to_z = [{"depth": d, "row": row, "col": z_at(w) * 2 + yh} for w in WAYS]
    to_x = [{"depth": d, "row": yl * X + x_at(w), "col": col} for w in WAYS]
    to_zy = [{"depth": d, "row": row, "col": z_at(w) * 2 + (1 - yh)} for w in WAYS]
    yh_peer = {"depth": d, "row": row, "col": z * 2 + (1 - yh)}
    yl_peer = {"depth": d, "row": (1 - yl) * X + x, "col": col}
    core_peer = {"depth": 1 - d, "row": row, "col": col}

    barrier = pltpu.get_barrier_semaphore()
    for peer in (*to_z, *to_x, yh_peer, yl_peer, core_peer):
        pl.semaphore_signal(barrier, inc=1, device_id=peer, device_id_type=MESH)

    mine_rows = pl.ds(pl.multiple_of(d * A_DATA, A_DATA), A_DATA)
    fetch_a = pltpu.make_async_copy(a_hbm.at[mine_rows, :], a_own, isem.at[0])
    fetch_b = pltpu.make_async_copy(b_hbm, b_own, isem.at[1])
    fetch_a.start()
    fetch_ai = pltpu.make_async_copy(ai_hbm, ai_ref, isem.at[2])
    fetch_bi = pltpu.make_async_copy(bi_hbm, bi_ref, isem.at[3])
    fetch_ci = pltpu.make_async_copy(ci_hbm, ci_ref, isem.at[4])
    fetch_ai.start()
    fetch_b.start()
    fetch_bi.start()
    fetch_ci.start()
    left = lax.broadcasted_iota(jnp.int32, (1, LANES), 1) < BS
    total[...] = jnp.zeros_like(total)

    fetch_a.wait()
    fetch_ai.wait()
    for m in range(MINE):
        x0 = a_own[pl.ds(m * BS, 32, stride=2), :]
        x1 = a_own[pl.ds(m * BS + 1, 32, stride=2), :]
        low, high = halves(x0, x1, left)
        abuf[z, yh, m * BS : m * BS + 32, :] = low
        abuf[z, yh, m * BS + 32 : m * BS + 64, :] = high
        for s in range(2):
            v = jnp.full((1, LANES), ai_ref[s, d * MINE + m])
            v = jnp.where(v < 0, -1, v + 1).astype(jnp.float32)
            r = A_DATA + m * 2 + s
            abuf[z, yh, r : r + 1, :] = v
    pl.semaphore_wait(barrier, 7)

    a_y = (yh, 1 - yh)
    b_y = (yl, 1 - yl)

    def remote(view, to, send, recv):
        return pltpu.make_async_remote_copy(
            src_ref=view, dst_ref=view, send_sem=send, recv_sem=recv,
            device_id=to, device_id_type=MESH,
        )

    started = []

    def start(copy):
        copy.start()
        started.append(copy)

    def a_view(e, k, sub, part):
        return abuf.at[z_at(-WAYS[e] * k), a_y[sub], pl.ds(*A_PARTS[part]), :]

    def a_next(e, k, sub, part):
        view = a_view(e, k, sub, part)
        start(remote(view, to_z[e], asend.at[e, k, sub, part], arecv.at[e, k + 1, sub, part]))

    def a_swap(part):
        view = a_view(0, 0, 0, part)
        start(remote(view, yh_peer, asend.at[0, 4, 0, part], arecv.at[0, 0, 1, part]))

    def a_across(e, part):
        view = a_view(0, 0, 0, part)
        start(remote(view, to_zy[e], asend.at[e, 0, 1, part], arecv.at[e, 1, 1, part]))

    def a_wait(e, k, sub, part):
        view = a_view(e, k, sub, part)
        remote(view, to_z[e], asend.at[e, 0, 0, 0], arecv.at[e, k, sub, part]).wait_recv()

    def a_over(e, k, part):
        view = a_view(e, k, 0, part)
        start(remote(view, yh_peer, asend.at[e, k, 1, part], arecv.at[e, k, 1, part]))

    def a_step(k, sub, i):
        for e in range(2):
            part = i if sub else (e + i) % 2
            a_wait(e, k, sub, part)
            if k < 3 or (k == 3 and part == e):
                a_next(e, k, sub, part)

    def a_other(part):
        a_wait(0, 0, 1, part)
        for e in range(2):
            a_next(e, 0, 1, part)

    def a_last(sub):
        for e in range(2):
            a_wait(e, 4, sub, e)
            if sub == 0:
                a_over(e, 4, e)

    def a_far(k):
        for e in range(2):
            for part in range(2):
                a_wait(e, k, 1, part)

    def b_view(chunk, half, part):
        first, size = B_PARTS[part]
        return bbuf.at[chunk, pl.ds(half * B_HALF + first, size)]

    def b_chunk(e, k, sub):
        return b_y[sub] * X + x_at(-WAYS[e] * k)

    def b_next(e, k, sub, part):
        view = b_view(b_chunk(e, k, sub), d, part)
        start(remote(view, to_x[e], bsend.at[e, k, sub, part], brecv.at[e, k + 1, sub, part]))

    def b_swap(part):
        view = b_view(b_chunk(0, 0, 0), d, part)
        start(remote(view, yl_peer, bsend.at[0, 2, 0, part], brecv.at[0, 0, 1, part]))

    def b_take(e, k, sub, part):
        chunk = b_chunk(e, k, sub)
        view = b_view(chunk, d, part)
        remote(view, to_x[e], bsend.at[e, 0, 0, part], brecv.at[e, k, sub, part]).wait_recv()
        start(remote(view, core_peer, fsend.at[chunk, part], frecv.at[chunk, part]))

    def b_step(sub, i):
        for e in range(2):
            part = i if sub else (e + i) % 2
            b_take(e, 1, sub, part)
            if part == e and sub == 0:
                b_next(e, 1, sub, part)

    def b_other(part):
        b_take(0, 0, 1, part)
        for e in range(2):
            b_next(e, 0, 1, part)

    def b_over(e):
        view = b_view(b_chunk(e, 2, 0), d, e)
        start(remote(view, yl_peer, bsend.at[e, 2, 1, e], brecv.at[e, 2, 1, e]))

    def b_last(sub):
        for e in range(2):
            b_take(e, 2, sub, e)
            if sub == 0:
                b_over(e)

    def b_shared():
        for k in range(X):
            for sub in range(2):
                if (k, sub) != (0, 0):
                    chunk = b_chunk(0, k, sub)
                    for part in range(2):
                        view = b_view(chunk, 1 - d, part)
                        remote(view, core_peer, fsend.at[chunk, part], frecv.at[chunk, part]).wait_recv()

    column = lax.broadcasted_iota(jnp.int32, (8, LANES), 0)

    def split(value):
        high = value.astype(jnp.bfloat16)
        return high, (value - high.astype(jnp.float32)).astype(jnp.bfloat16)

    def wide(mask):
        row = jnp.where(mask, 1.0, 0.0)
        return jnp.broadcast_to(row, (BS, LANES)).astype(jnp.bfloat16) > 0

    def tile(new, k, m):
        zs = z_at(k)
        base = pl.multiple_of(m * BS, BS)
        wanted = [ci_ref[t, d * MINE + m] for t in range(4)]
        lhs = jnp.concatenate([abuf[zs, y, pl.ds(base, BS), :] for y in range(2)], axis=1)
        tags = [abuf[zs, y, pl.ds(A_DATA + m * 2 + s, 1), :] for y in range(2) for s in range(2)]
        sides = []
        for p in range(2):
            got, ids = [], []
            for t in (2 * p, 2 * p + 1):
                n = jnp.maximum(wanted[t], 0)
                got.append(bbuf[zs, pl.ds(n * 8 + 1, 8)].reshape(BS, LANES))
                tag = jnp.where(column == wanted[t], bbuf[zs, TAGS[0], 0:8, :], 0.0)
                tag += jnp.where(column + 8 == wanted[t], bbuf[zs, TAGS[1], 0:8, :], 0.0)
                ids.append(jnp.sum(tag, axis=0, keepdims=True))
            straight = jnp.where(left, got[0], got[1])
            crossed = pltpu.roll(jnp.where(left, got[1], got[0]), BS, 1)
            tag_straight = jnp.where(left, ids[0], ids[1])
            tag_crossed = pltpu.roll(jnp.where(left, ids[1], ids[0]), BS, 1)
            straight, crossed = split(straight), split(crossed)
            masks = [(wide(t == tag_straight), wide(t == tag_crossed)) for t in tags]
            zero = jnp.zeros((BS, LANES), jnp.bfloat16)
            sides.append([
                jnp.concatenate([
                    jnp.where(here, straight[i], jnp.where(there, crossed[i], zero))
                    for here, there in masks
                ], axis=0)
                for i in range(2)
            ])
        r_hi, r_lo = (jnp.concatenate([side[i] for side in sides], axis=1) for i in range(2))
        l_hi, l_lo = split(lhs)
        low = jnp.dot(l_hi, r_lo, preferred_element_type=jnp.float32)
        both = jnp.concatenate([l_hi, l_lo], axis=0)
        both = jnp.dot(both, r_hi, preferred_element_type=jnp.float32)
        return new + ((low + both[BS:]) + both[:BS])

    def summed(m, panels):
        new = total[m]
        for k in panels:
            new = tile(new, k, m)
        return new

    def tiles(*panels):
        def body(m, carry):
            total[m] = summed(m, panels)
            return carry

        lax.fori_loop(0, MINE, body, 0)

    a_swap(0)
    for i in range(2):
        for e in range(2):
            a_next(e, 0, 0, (e + i) % 2)
    fetch_b.wait()
    fetch_bi.wait()
    fetch_ci.wait()
    for n in range(COLS):
        x0 = b_own[pl.ds(n * BS, 32, stride=2), :]
        x1 = b_own[pl.ds(n * BS + 1, 32, stride=2), :]
        low, high = halves(x0, x1, left)
        for g in range(8):
            group = 1 + n * 8 + g
            bbuf[row, group, pl.ds(0, 4, stride=2), :] = low[g * 4 : g * 4 + 4]
            bbuf[row, group, pl.ds(1, 4, stride=2), :] = high[g * 4 : g * 4 + 4]
        v0 = jnp.full((1, LANES), bi_ref[0, n])
        v1 = jnp.full((1, LANES), bi_ref[1, n])
        v = (jnp.where(left, v0, v1) + 1).astype(jnp.float32)
        r = n % 8
        bbuf[row, TAGS[n // 8], r : r + 1, :] = v

    b_swap(0)
    a_swap(1)
    b_swap(1)
    for i in range(2):
        for e in range(2):
            b_next(e, 0, 0, (e + i) % 2)
    a_step(1, 0, 0)
    a_other(0)
    a_step(1, 0, 1)
    b_step(0, 0)
    b_other(0)
    a_step(2, 0, 0)
    b_step(0, 1)
    a_other(1)
    b_other(1)
    a_step(2, 0, 1)
    a_step(1, 1, 0)
    b_last(0)
    a_step(3, 0, 0)
    a_step(1, 1, 1)
    b_step(1, 0)
    a_step(3, 0, 1)
    b_step(1, 1)
    a_step(2, 1, 0)
    a_last(0)
    b_last(1)
    a_step(2, 1, 1)
    b_shared()
    tiles(0, 1, -1, 2, -2)
    a_far(3)
    a_last(1)

    def c_copy(m):
        at = pl.ds(pl.multiple_of((d * MINE + m) * LANES, LANES), LANES)
        return remote(o_ref.at[at, :], core_peer, csend.at[m], crecv.at[m])

    def last(m, carry):
        done = summed(m, (3, -3, 4))
        out = pl.multiple_of((d * MINE + m) * LANES, LANES)
        for p in range(2):
            v0 = done[:32, p * LANES : (p + 1) * LANES]
            v1 = done[32:, p * LANES : (p + 1) * LANES]
            low, high = halves(v0, v1, left)
            o_ref[pl.ds(out + 2 * p, 32, stride=4), :] = low
            o_ref[pl.ds(out + 2 * p + 1, 32, stride=4), :] = high
        c_copy(m).start()
        return carry

    lax.fori_loop(0, MINE, last, 0)

    for copy in started:
        copy.wait_send()
    for m in range(MINE):
        at = pl.ds(pl.multiple_of(((1 - d) * MINE + m) * LANES, LANES), LANES)
        remote(o_ref.at[at, :], core_peer, csend.at[m], crecv.at[m]).wait_recv()
        c_copy(m).wait_send()


def interleaved(blocks):
    r, s, _ = blocks.shape
    return blocks.reshape(r, s, 32, LANES).transpose(0, 2, 1, 3).reshape(r * 32 * s, LANES)


def per_device(a_blocks, a_index, b_blocks, b_index, c_index):
    vmem = pl.BlockSpec(memory_space=pltpu.VMEM)
    hbm = pl.BlockSpec(memory_space=pltpu.HBM)
    dma = pltpu.SemaphoreType.DMA
    out = pl.pallas_call(
        kernel,
        out_shape=pltpu.VMEM((ROWS * LANES, LANES), jnp.float32),
        in_specs=[hbm] * 5,
        out_specs=vmem,
        scratch_shapes=[
            pltpu.SMEM((2, ROWS), jnp.int32),
            pltpu.SMEM((2, COLS), jnp.int32),
            pltpu.SMEM((4, ROWS), jnp.int32),
            pltpu.VMEM((A_DATA, LANES), jnp.float32),
            pltpu.VMEM((COLS * BS, LANES), jnp.float32),
            pltpu.VMEM((Z, 2, A_PIECE, LANES), jnp.float32),
            pltpu.VMEM((2 * X, 2 * B_HALF, GROUP, LANES), jnp.float32),
            pltpu.VMEM((MINE, BS, 4 * BS), jnp.float32),
            dma((5,)),
            dma((2, 5, 2, 2)),
            dma((2, 5, 2, 2)),
            dma((2, 3, 2, 2)),
            dma((2, 3, 2, 2)),
            dma((2 * X, 2)),
            dma((2 * X, 2)),
            dma((MINE,)),
            dma((MINE,)),
        ],
        compiler_params=pltpu.CompilerParams(
            collective_id=0, has_side_effects=True, vmem_limit_bytes=56 << 20
        ),
    )(interleaved(a_blocks), a_index.T, interleaved(b_blocks), b_index.T, c_index.T)
    return out.reshape(ROWS, 32, 4, LANES).transpose(0, 2, 1, 3).reshape(ROWS, 4, BS * BS)


def solution(mesh):
    placed = (
        P("row", "col", None),
        P("row", "col"),
        P("col", "row", None),
        P("col", "row"),
        P("row", "col"),
    )
    return jax.shard_map(
        per_device, mesh=mesh, in_specs=placed, out_specs=P("row", "col", None), check_vma=False
    )
```
